32 devices in a mesh: gx: 8 (over z, x), gy: 4 (over y, core).
Axes of the slice: x: 2, y: 2, z: 4, core: 2. Of those that a mesh axis runs over, the one named last changes fastest.
Arguments:
- source_snaps: float32 [4, 384, 64, 256], P(None, 'gx', 'gy'), may hold values from -6 to 6
- receiver_snaps: float32 [4, 384, 64, 256], P(None, 'gx', 'gy'), may hold values from -6 to 6
- snap_pairs: int32 [3, 2], replicated, may hold values from 0 to 3
- offset_lags: int32 [17], replicated, may hold values from -24 to 24, as said below
- weight_table: float32 [4, 17], replicated, may hold values from 0.2 to 1
- weight_index: int32 [3], replicated, may hold values from 0 to 3
Outputs:
- adjoint_source: float32 [3, 384, 64, 256], P(None, 'gx', 'gy')
- adjoint_receiver: float32 [3, 384, 64, 256], P(None, 'gx', 'gy')
The draws below stay inside these ranges and needn't reach their ends.
Inputs may be any that keep to these rules, and one draw needn't show every extreme that they name: `offset_lags`: strictly increasing; the first entry is -24 and the last is 24.
All inputs are finite; a program needn't handle non-finite values.
Results may differ from the reference program's by a relative error of at most 0.00002.
Values sent between devices are 32-bit elements; how exact they have to be, the bound alone decides.
A program may use at most 128 MiB of HBM per device.

```python
import jax
import jax.numpy as jnp
from jax import lax

NZ = 256
NSNAP = 4
PAIRS = 3
NOFF = 17
MAXLAG = 24
NW = 4
NX = 384
NY = 64


def draw_offset_lags(key, part):
    ramp = jnp.arange(NOFF, dtype=jnp.int32)
    base = -MAXLAG + ramp * (2 * MAXLAG) // (NOFF - 1)
    jitter = jax.random.randint(key, (NOFF,), -1, 2, dtype=jnp.int32)
    inner = (ramp > 0) & (ramp < NOFF - 1)
    return (base + jnp.where(inner, jitter, 0)).astype(jnp.int32)


def with_ends(drawn, key, smallest, largest):
    extent = drawn.shape
    spot = [jax.random.randint(jax.random.fold_in(key, axis), (), 0, extent[axis]) for axis in range(len(extent))]
    drawn = drawn.at[tuple(spot)].set(smallest)
    longest = extent.index(max(extent))
    spot[longest] = (spot[longest] + 1) % extent[longest]
    return drawn.at[tuple(spot)].set(largest)


def shard_levels(rng, dims, split, least, high):
    def one(axis_at, parts):
        draws = jax.random.uniform(jax.random.fold_in(jax.random.fold_in(rng, 6), axis_at), (parts,), jnp.float32, least / len(split), high / len(split))
        return jnp.repeat(jnp.exp(draws), dims[axis_at] // parts).reshape((-1,) + (1,) * (len(dims) - axis_at - 1))

    factor_of = one(*split[0])
    for cut in split[1:]:
        factor_of = factor_of * one(*cut)
    return factor_of


def scatter_about(key, dims, deviation, most, cuts=(), held_as=jnp.bfloat16):
    values = jax.random.normal(key, dims, jnp.float32) * deviation
    if len(cuts) > 0:
        values = shard_levels(key, dims, cuts, -0.22, 0.18) * values
    return jnp.clip(values, min=-most, max=most).astype(held_as)


def setup_inputs(seed: int = 0) -> dict:
    keys = jax.random.split(jax.random.key(seed), 7)
    return {
        "source_snaps": scatter_about(keys[0], (NSNAP, NX, NY, NZ), 1.0, 6.0, ((1, 8), (2, 4)), jnp.float32),
        "receiver_snaps": scatter_about(keys[1], (NSNAP, NX, NY, NZ), 1.0, 6.0, ((1, 8), (2, 4)), jnp.float32),
        "snap_pairs": with_ends(jax.random.randint(keys[2], (PAIRS, 2), 0, NSNAP), jax.random.fold_in(keys[2], 1), 0, NSNAP - 1).astype(jnp.int32),
        "offset_lags": draw_offset_lags(jax.random.fold_in(keys[6], 71), 0),
        "weight_table": jnp.clip(jax.random.uniform(keys[4], (NW, NOFF), jnp.float32, 0.2, 1.0), 0.2, 1.0),
        "weight_index": jax.random.randint(keys[5], (PAIRS,), 0, NW).astype(jnp.int32),
    }


def smooth(values):
    return (values[:, :-4] + values[:, 4:] + 4.0 * (values[:, 1:-3] + values[:, 3:-1]) + 6.0 * values[:, 2:-2]) / 16.0


def reference(source_snaps, receiver_snaps, snap_pairs, offset_lags, weight_table, weight_index):
    source_list = []
    receiver_list = []
    for pair_index in range(PAIRS):
        source_field = source_snaps[snap_pairs[pair_index, 0]]
        receiver_field = receiver_snaps[snap_pairs[pair_index, 1]]
        source_pad = jnp.pad(source_field, ((2 * MAXLAG, 2 * MAXLAG), (2, 2), (0, 0)))
        receiver_pad = jnp.pad(receiver_field, ((2 * MAXLAG, 2 * MAXLAG), (2, 2), (0, 0)))
        weights = weight_table[weight_index[pair_index]]

        def step(offset, running):
            source_total, receiver_total = running
            offset_lag = offset_lags[offset]
            weight = weights[offset]
            shifted_source = lax.dynamic_slice_in_dim(source_pad, 2 * MAXLAG - offset_lag, NX, 0)
            shifted_receiver = lax.dynamic_slice_in_dim(receiver_pad, 2 * MAXLAG + offset_lag, NX, 0)
            smoothed = smooth(weight * shifted_source * shifted_receiver)
            smoothed_pad = jnp.pad(smoothed, ((MAXLAG, MAXLAG), (0, 0), (0, 0)))
            far_receiver = lax.dynamic_slice_in_dim(receiver_pad, 2 * MAXLAG + 2 * offset_lag, NX, 0)[:, 2:-2]
            far_source = lax.dynamic_slice_in_dim(source_pad, 2 * MAXLAG - 2 * offset_lag, NX, 0)[:, 2:-2]
            source_total = source_total + lax.dynamic_slice_in_dim(smoothed_pad, MAXLAG + offset_lag, NX, 0) * far_receiver
            receiver_total = receiver_total + lax.dynamic_slice_in_dim(smoothed_pad, MAXLAG - offset_lag, NX, 0) * far_source
            return (source_total, receiver_total)

        zeros = jnp.zeros(source_field.shape, jnp.float32)
        source_total, receiver_total = lax.fori_loop(0, NOFF, step, (zeros, zeros))
        source_list.append(source_total)
        receiver_list.append(receiver_total)
    return (jnp.stack(source_list), jnp.stack(receiver_list))
```

```python
import functools

import jax
import jax.numpy as jnp
from jax import lax
from jax.experimental import pallas as pl
from jax.experimental.pallas import tpu as pltpu
from jax.sharding import PartitionSpec as P


SUB = 8
RADIUS = 2


def smooth_rows(rows):
    for _ in range(2 * RADIUS):
        rows = [low + high for low, high in zip(rows[:-1], rows[1:])]
    return rows


def adjoint_kernel(
    cells_x, cells_y, scalars, lags, weights, own, recv, near, far, below, above, out, wide
):
    parity = scalars[0]
    row = scalars[1]
    noff = lags.shape[0]
    blocks = cells_x // SUB
    starts = (
        cells_x + cells_x * parity,
        2 * cells_x - cells_x * parity,
        3 * cells_x - 3 * cells_x * parity,
        3 * cells_x * parity,
    )

    for piece, (ref, start) in enumerate(zip((own, recv, near, far), starts)):
        for field in range(2):

            @pl.loop(0, blocks)
            def _(block):
                at = pl.ds(pl.multiple_of(start + block * SUB, SUB), SUB)
                first = block * SUB
                for y in range(cells_y):
                    wide[field, y + RADIUS, at, :] = ref[
                        field, pl.ds(first * cells_y + y, SUB, stride=cells_y), :
                    ]
                for y in range(RADIUS):
                    edge = pl.ds((piece * cells_x + first) * RADIUS + y, SUB, stride=RADIUS)
                    wide[field, y, at, :] = below[field, edge, :]
                    wide[field, cells_y + RADIUS + y, at, :] = above[field, edge, :]

    for field in range(2):
        sign = 2 if field == 0 else -2

        @pl.loop(0, 2 * blocks)
        def _(block):
            base = cells_x + block * SUB
            at = pl.ds(pl.multiple_of(base, SUB), SUB)
            rows = cells_y + 2 * RADIUS
            centre = [wide[field, y, at, :] for y in range(rows)]

            def step(h, totals):
                moved = pl.ds(base + sign * lags[h], SUB)
                weight = weights[row, h] * 0.0625
                other = [wide[1 - field, y, moved, :] for y in range(rows)]
                image = smooth_rows([c * o for c, o in zip(centre, other)])
                return tuple(
                    total + (weight * value) * o
                    for total, value, o in zip(totals, image, other[RADIUS:])
                )

            zeros = tuple(jnp.zeros((SUB, 128), jnp.float32) for _ in range(cells_y))
            totals = lax.fori_loop(0, noff, step, zeros)
            upper = (block >= blocks).astype(jnp.int32)
            side = upper + parity - 2 * upper * parity
            first = (block - upper * blocks) * SUB * cells_y
            for y in range(cells_y):
                out[side, field, pl.ds(first + y, SUB, stride=cells_y), :] = totals[y]


def adjoints(scalars, lags, weights, own, recv, near, far, below, above):
    _, cells_x, cells_y, lanes = own.shape

    def flat(a):
        return a.reshape(2, -1, lanes)

    smem = pl.BlockSpec(memory_space=pltpu.SMEM)
    vmem = pl.BlockSpec(memory_space=pltpu.VMEM)
    out = pl.pallas_call(
        functools.partial(adjoint_kernel, cells_x, cells_y),
        out_shape=jax.ShapeDtypeStruct((2, 2, cells_x * cells_y, lanes), jnp.float32),
        in_specs=[smem] * 3 + [vmem] * 6,
        out_specs=vmem,
        scratch_shapes=[
            pltpu.VMEM((2, cells_y + 2 * RADIUS, 4 * cells_x, lanes), jnp.float32)
        ],
        cost_estimate=pl.CostEstimate(
            flops=60_000_000, bytes_accessed=12_000_000, transcendentals=0
        ),
        compiler_params=pltpu.CompilerParams(vmem_limit_bytes=32 * 1024 * 1024),
        name="adjoints",
    )(scalars, lags, weights, *map(flat, (own, recv, near, far, below, above)))
    return out.reshape(2, 2, cells_x, cells_y, lanes)


def local(source_snaps, receiver_snaps, snap_pairs, offset_lags, weight_table, weight_index):
    _, cells_x, cells_y, depth = source_snaps.shape
    lanes = depth // 2
    pair_count = snap_pairs.shape[0]
    gx = lax.axis_size("gx")
    gy = lax.axis_size("gy")
    parity = lax.rem(lax.axis_index("gx"), 2)

    swap = [(i, i ^ 1) for i in range(gx)]
    outward = [(i, i - 2 if i % 2 == 0 else i + 2) for i in range(gx)]
    outward = [(i, j) for i, j in outward if 0 <= j < gx]
    inward = [(i, i + 2 if i % 2 == 0 else i - 2) for i in range(gx)]
    inward = [(i, j) for i, j in inward if 0 <= j < gx]
    up = [(i, i + 1) for i in range(gy - 1)]
    down = [(j, i) for i, j in up]

    def half(pair, side):
        size = (1, cells_x, cells_y, lanes)
        return jnp.concatenate(
            [
                lax.dynamic_slice(source_snaps, (snap_pairs[pair, 0], 0, 0, side * lanes), size),
                lax.dynamic_slice(receiver_snaps, (snap_pairs[pair, 1], 0, 0, side * lanes), size),
            ],
            axis=0,
        )

    pieces = []
    for pair in range(pair_count):
        recv = lax.ppermute(half(pair, 1 - parity), "gx", swap)
        own = half(pair, parity)
        near = lax.ppermute(own, "gx", outward)
        far = lax.ppermute(recv, "gx", inward)
        pieces.append((own, recv, near, far))

    results = []
    for pair in range(pair_count):
        group = pieces[pair]

        def edge(start):
            rows = [lax.slice_in_dim(a, start, start + RADIUS, axis=2) for a in group]
            return jnp.stack(rows, axis=1)

        below = lax.ppermute(edge(cells_y - RADIUS), "gy", up)
        above = lax.ppermute(edge(0), "gy", down)
        scalars = jnp.stack([parity.astype(jnp.int32), weight_index[pair]])
        out = adjoints(scalars, offset_lags, weight_table, *group, below, above)
        results.append((out[0], lax.ppermute(out[1], "gx", swap)))

    whole = []
    for mine, theirs in results:
        low = jnp.where(parity == 0, mine, theirs)
        high = jnp.where(parity == 0, theirs, mine)
        whole.append(jnp.concatenate([low, high], axis=-1))
    whole = jnp.stack(whole, axis=1)
    return whole[0], whole[1]


def solution(mesh):
    return jax.shard_map(
        local,
        mesh=mesh,
        in_specs=(P(None, "gx", "gy", None), P(None, "gx", "gy", None), P(), P(), P(), P()),
        out_specs=(P(None, "gx", "gy", None), P(None, "gx", "gy", None)),
        check_vma=False,
    )
```

```python
import functools

import jax
import jax.numpy as jnp
from jax import lax
from jax.experimental import pallas as pl
from jax.experimental.pallas import tpu as pltpu
from jax.sharding import PartitionSpec as P

SUB = 8
LANES = 128
RADIUS = 2
MESH = pl.DeviceIdType.MESH
SWAP, NEAR, FAR, REST_UP, REST_DOWN, FAR_UP, FAR_DOWN, OUT = range(8)
KINDS = OUT + 2


def smooth_rows(rows):
    for _ in range(2 * RADIUS):
        rows = [low + high for low, high in zip(rows[:-1], rows[1:])]
    return rows


def gather_kernel(pairs, source, receiver, own, sent):
    parity = lax.rem(lax.axis_index("gx"), 2)
    for field, ref in enumerate((source, receiver)):
        for out, side in ((own, parity), (sent, 1 - parity)):
            at = pl.ds(pl.multiple_of(side * LANES, LANES), LANES)
            out[0, field] = jnp.swapaxes(ref[0, :, :, at], 0, 1)


def gather(snap_pairs, source_snaps, receiver_snaps):
    _, cells_x, cells_y, depth = source_snaps.shape
    pair_count = snap_pairs.shape[0]
    block = (1, cells_x, cells_y, depth)
    shape = (2, cells_y, cells_x, LANES)
    out = pl.BlockSpec((1, *shape), lambda p, pairs: (p, 0, 0, 0, 0))
    return pl.pallas_call(
        gather_kernel,
        out_shape=[jax.ShapeDtypeStruct((pair_count, *shape), jnp.float32)] * 2,
        grid_spec=pltpu.PrefetchScalarGridSpec(
            num_scalar_prefetch=1,
            grid=(pair_count,),
            in_specs=[
                pl.BlockSpec(block, lambda p, pairs: (pairs[p, 0], 0, 0, 0)),
                pl.BlockSpec(block, lambda p, pairs: (pairs[p, 1], 0, 0, 0)),
            ],
            out_specs=[out, out],
        ),
        compiler_params=pltpu.CompilerParams(vmem_limit_bytes=16 * 1024 * 1024),
        name="gather",
    )(snap_pairs, source_snaps, receiver_snaps)


def adjoint_kernel(
    gx, gy, lags, weights, rows_of, own, sent, out_s, out_r, *scratch
):
    pair_count = own.shape[0]
    cells_y, cells_x = own.shape[2:4]
    wides = scratch[:pair_count]
    stages = scratch[pair_count : 2 * pair_count]
    send_sem, recv_sem, own_sem, mine_sem = scratch[2 * pair_count :]
    outs = (out_s, out_r)
    noff = lags.shape[0]
    blocks = cells_x // SUB

    ix = lax.axis_index("gx")
    iy = lax.axis_index("gy")
    parity = lax.rem(ix, 2)
    partner = ix + 1 - 2 * parity
    outward = ix - 2 + 4 * parity
    inward = ix + 2 - 4 * parity
    has_out = (outward >= 0) & (outward < gx)
    has_in = (inward >= 0) & (inward < gx)
    has_low = iy > 0
    has_high = iy < gy - 1

    own_at = pl.ds(pl.multiple_of(cells_x + cells_x * parity, SUB), cells_x)
    recv_at = pl.ds(pl.multiple_of(2 * cells_x - cells_x * parity, SUB), cells_x)
    near_at = pl.ds(pl.multiple_of(3 * cells_x - 3 * cells_x * parity, SUB), cells_x)
    far_at = pl.ds(pl.multiple_of(3 * cells_x * parity, SUB), cells_x)
    rest_at = pl.ds(pl.multiple_of(cells_x - cells_x * parity, SUB), 3 * cells_x)
    core = pl.ds(RADIUS, cells_y)
    lane_at = pl.ds(pl.multiple_of(parity * LANES, LANES), LANES)

    barrier = pltpu.get_barrier_semaphore()

    def greet(axis, index):
        pl.semaphore_signal(barrier, inc=1, device_id={axis: index}, device_id_type=MESH)

    greet("gx", partner)
    pl.when(has_out)(lambda: greet("gx", outward))
    pl.when(has_in)(lambda: greet("gx", inward))
    pl.when(has_low)(lambda: greet("gy", iy - 1))
    pl.when(has_high)(lambda: greet("gy", iy + 1))

    for wide in wides:
        for field in range(2):

            @pl.when(jnp.logical_not(has_in))
            def _():
                wide[field, core, near_at, :] = jnp.zeros((cells_y, cells_x, LANES), jnp.float32)

            @pl.when(jnp.logical_not(has_out))
            def _():
                wide[field, core, far_at, :] = jnp.zeros((cells_y, cells_x, LANES), jnp.float32)

            edge = jnp.zeros((RADIUS, 4 * cells_x, LANES), jnp.float32)

            @pl.when(jnp.logical_not(has_low))
            def _():
                wide[field, pl.ds(0, RADIUS)] = edge

            @pl.when(jnp.logical_not(has_high))
            def _():
                wide[field, pl.ds(cells_y + RADIUS, RADIUS)] = edge

    pl.semaphore_wait(
        barrier,
        1 + sum(flag.astype(jnp.int32) for flag in (has_out, has_in, has_low, has_high)),
    )

    def remote(pair, kind, src, dst, axis, index):
        return pltpu.make_async_remote_copy(
            src_ref=src,
            dst_ref=dst,
            send_sem=send_sem.at[pair, kind],
            recv_sem=recv_sem.at[pair, kind],
            device_id={axis: index},
            device_id_type=MESH,
        )

    def swap_copy(pair):
        dst = wides[pair].at[:, core, own_at, :]
        return remote(pair, SWAP, sent.at[pair], dst, "gx", partner)

    def swap_arrival(pair):
        dst = wides[pair].at[:, core, recv_at, :]
        return remote(pair, SWAP, sent.at[pair], dst, "gx", partner)

    def near_copy(pair):
        return remote(
            pair, NEAR, own.at[pair], wides[pair].at[:, core, near_at, :], "gx", outward
        )

    def far_copy(pair):
        wide = wides[pair]
        return remote(
            pair,
            FAR,
            wide.at[:, core, recv_at, :],
            wide.at[:, core, far_at, :],
            "gx",
            inward,
        )

    def edge_copies(pair, kind, at):
        wide = wides[pair]
        size = RADIUS
        up = remote(
            pair,
            kind,
            wide.at[:, pl.ds(cells_y, size), at, :],
            wide.at[:, pl.ds(0, size), at, :],
            "gy",
            iy + 1,
        )
        down = remote(
            pair,
            kind + 1,
            wide.at[:, pl.ds(RADIUS, size), at, :],
            wide.at[:, pl.ds(cells_y + RADIUS, size), at, :],
            "gy",
            iy - 1,
        )
        return up, down

    def start_edges(pair, kind, at):
        up, down = edge_copies(pair, kind, at)
        pl.when(has_high)(up.start)
        pl.when(has_low)(down.start)

    def wait_edges(pair, kind, at):
        up, down = edge_copies(pair, kind, at)
        pl.when(has_low)(up.wait_recv)
        pl.when(has_high)(down.wait_recv)

    def own_copy(pair):
        return pltpu.make_async_copy(
            own.at[pair], wides[pair].at[:, core, own_at, :], own_sem.at[pair]
        )

    def out_copy(pair, field):
        return remote(
            pair,
            OUT + field,
            stages[pair].at[1, field],
            outs[field].at[pair, :, lane_at],
            "gx",
            partner,
        )

    def out_arrival(pair, field):
        theirs = pl.ds(pl.multiple_of((1 - parity) * LANES, LANES), LANES)
        return remote(
            pair,
            OUT + field,
            stages[pair].at[1, field],
            outs[field].at[pair, :, theirs],
            "gx",
            partner,
        )

    def mine_copy(pair, field):
        return pltpu.make_async_copy(
            stages[pair].at[0, field],
            outs[field].at[pair, :, lane_at],
            mine_sem.at[pair, field],
        )

    def compute(pair, side):
        wide, stage = wides[pair], stages[pair]
        rows = cells_y + 2 * RADIUS
        row = rows_of[pair]
        upper = side + parity - 2 * side * parity

        @pl.loop(0, 2 * blocks)
        def _(step):
            field = step // blocks
            block = step - field * blocks
            sign = 2 - 4 * field
            base = cells_x + upper * cells_x + block * SUB
            at = pl.ds(pl.multiple_of(base, SUB), SUB)
            centre = [wide[field, y, at, :] for y in range(rows)]

            def term(h, totals):
                moved = pl.ds(base + sign * lags[h], SUB)
                weight = weights[row, h] * 0.0625
                other = [wide[1 - field, y, moved, :] for y in range(rows)]
                image = smooth_rows([c * o for c, o in zip(centre, other)])
                return tuple(
                    total + (weight * value) * o
                    for total, value, o in zip(totals, image, other[RADIUS:])
                )

            zeros = tuple(jnp.zeros((SUB, LANES), jnp.float32) for _ in range(cells_y))
            totals = lax.fori_loop(0, noff, term, zeros)
            first = block * SUB * cells_y
            for y in range(cells_y):
                stage[side, field, pl.ds(first + y, SUB, stride=cells_y), :] = totals[y]

    pairs = range(pair_count)
    for pair in pairs:
        swap_copy(pair).start()
        pl.when(has_out)(near_copy(pair).start)
    for pair in pairs:
        own_copy(pair).start()
    for pair in pairs:
        own_copy(pair).wait()

    def forward(pair):
        swap_arrival(pair).wait_recv()
        pl.when(has_in)(far_copy(pair).start)
        pl.when(has_in)(near_copy(pair).wait_recv)
        start_edges(pair, REST_UP, rest_at)

    def finish(pair):
        pl.when(has_out)(far_copy(pair).wait_recv)
        start_edges(pair, FAR_UP, far_at)

    def settle(pair):
        wait_edges(pair, REST_UP, rest_at)
        wait_edges(pair, FAR_UP, far_at)

    forward(0)
    for pair in pairs:
        if pair + 1 < pair_count:
            forward(pair + 1)
        finish(pair)
        settle(pair)
        compute(pair, 1)
        for field in range(2):
            out_copy(pair, field).start()
        compute(pair, 0)
        for field in range(2):
            mine_copy(pair, field).start()

    for pair in pairs:
        swap_copy(pair).wait_send()
        pl.when(has_out)(near_copy(pair).wait_send)
        pl.when(has_in)(far_copy(pair).wait_send)
        for kind, at in ((REST_UP, rest_at), (FAR_UP, far_at)):
            up, down = edge_copies(pair, kind, at)
            pl.when(has_high)(up.wait_send)
            pl.when(has_low)(down.wait_send)
        for field in range(2):
            mine_copy(pair, field).wait()
            out_copy(pair, field).wait_send()
            out_arrival(pair, field).wait_recv()


def local(source_snaps, receiver_snaps, snap_pairs, offset_lags, weight_table, weight_index):
    _, cells_x, cells_y, depth = source_snaps.shape
    pair_count = snap_pairs.shape[0]
    own, sent = gather(snap_pairs, source_snaps, receiver_snaps)
    smem = pl.BlockSpec(memory_space=pltpu.SMEM)
    vmem = pl.BlockSpec(memory_space=pltpu.VMEM)
    anywhere = pl.BlockSpec(memory_space=pl.ANY)
    wide = pltpu.VMEM((2, cells_y + 2 * RADIUS, 4 * cells_x, LANES), jnp.float32)
    stage = pltpu.VMEM((2, 2, cells_x * cells_y, LANES), jnp.float32)
    out = pl.pallas_call(
        functools.partial(adjoint_kernel, lax.axis_size("gx"), lax.axis_size("gy")),
        out_shape=[
            jax.ShapeDtypeStruct((pair_count, cells_x * cells_y, depth), jnp.float32)
        ] * 2,
        in_specs=[smem] * 3 + [vmem] * 2,
        out_specs=[anywhere] * 2,
        scratch_shapes=[wide] * pair_count
        + [stage] * pair_count
        + [
            pltpu.SemaphoreType.DMA((pair_count, KINDS)),
            pltpu.SemaphoreType.DMA((pair_count, KINDS)),
            pltpu.SemaphoreType.DMA((pair_count,)),
            pltpu.SemaphoreType.DMA((pair_count, 2)),
        ],
        compiler_params=pltpu.CompilerParams(
            collective_id=0, has_side_effects=True, vmem_limit_bytes=48 * 1024 * 1024
        ),
        name="adjoints",
    )(offset_lags, weight_table, weight_index, own, sent)
    return tuple(a.reshape(pair_count, cells_x, cells_y, depth) for a in out)


def solution(mesh):
    return jax.shard_map(
        local,
        mesh=mesh,
        in_specs=(P(None, "gx", "gy", None), P(None, "gx", "gy", None), P(), P(), P(), P()),
        out_specs=(P(None, "gx", "gy", None), P(None, "gx", "gy", None)),
        check_vma=False,
    )
```

```python
import functools

import jax
import jax.numpy as jnp
from jax import lax
from jax.experimental import pallas as pl
from jax.experimental.pallas import tpu as pltpu
from jax.sharding import PartitionSpec as P

SUB = 8
LANES = 128
RADIUS = 2
MESH = pl.DeviceIdType.MESH
SWAP, NEAR, FAR, REST_UP, REST_DOWN, FAR_UP, FAR_DOWN, OUT = range(8)
KINDS = OUT + 2


def smooth_rows(rows):
    for _ in range(2 * RADIUS):
        rows = [low + high for low, high in zip(rows[:-1], rows[1:])]
    return rows


def gather_kernel(pairs, source, receiver, own, sent):
    parity = lax.rem(lax.axis_index("gx"), 2)
    for field, ref in enumerate((source, receiver)):
        for out, side in ((own, parity), (sent, 1 - parity)):
            at = pl.ds(pl.multiple_of(side * LANES, LANES), LANES)
            out[0, field] = jnp.swapaxes(ref[0, :, :, at], 0, 1)


def gather(snap_pairs, source_snaps, receiver_snaps):
    _, cells_x, cells_y, depth = source_snaps.shape
    pair_count = snap_pairs.shape[0]
    block = (1, cells_x, cells_y, depth)
    shape = (2, cells_y, cells_x, LANES)
    out = pl.BlockSpec((1, *shape), lambda p, pairs: (p, 0, 0, 0, 0))
    return pl.pallas_call(
        gather_kernel,
        out_shape=[jax.ShapeDtypeStruct((pair_count, *shape), jnp.float32)] * 2,
        grid_spec=pltpu.PrefetchScalarGridSpec(
            num_scalar_prefetch=1,
            grid=(pair_count,),
            in_specs=[
                pl.BlockSpec(block, lambda p, pairs: (pairs[p, 0], 0, 0, 0)),
                pl.BlockSpec(block, lambda p, pairs: (pairs[p, 1], 0, 0, 0)),
            ],
            out_specs=[out, out],
        ),
        compiler_params=pltpu.CompilerParams(vmem_limit_bytes=58 * 1024 * 1024),
        name="gather",
    )(snap_pairs, source_snaps, receiver_snaps)


def adjoint_kernel(
    gx, gy, lags, weights, rows_of, own, sent, out_s, out_r, *scratch
):
    pair_count = own.shape[0]
    cells_y, cells_x = own.shape[2:4]
    wides = scratch[:pair_count]
    stages = scratch[pair_count : 2 * pair_count]
    send_sem, recv_sem, own_sem, mine_sem = scratch[2 * pair_count :]
    outs = (out_s, out_r)
    noff = lags.shape[0]
    blocks = cells_x // SUB

    ix = lax.axis_index("gx")
    iy = lax.axis_index("gy")
    parity = lax.rem(ix, 2)
    partner = ix + 1 - 2 * parity
    outward = ix - 2 + 4 * parity
    inward = ix + 2 - 4 * parity
    has_out = (outward >= 0) & (outward < gx)
    has_in = (inward >= 0) & (inward < gx)
    has_low = iy > 0
    has_high = iy < gy - 1

    own_at = pl.ds(pl.multiple_of(cells_x + cells_x * parity, SUB), cells_x)
    recv_at = pl.ds(pl.multiple_of(2 * cells_x - cells_x * parity, SUB), cells_x)
    near_at = pl.ds(pl.multiple_of(3 * cells_x - 3 * cells_x * parity, SUB), cells_x)
    far_at = pl.ds(pl.multiple_of(3 * cells_x * parity, SUB), cells_x)
    rest_at = pl.ds(pl.multiple_of(cells_x - cells_x * parity, SUB), 3 * cells_x)
    core = pl.ds(RADIUS, cells_y)
    lane_at = pl.ds(pl.multiple_of(parity * LANES, LANES), LANES)

    barrier = pltpu.get_barrier_semaphore()

    def greet(axis, index):
        pl.semaphore_signal(barrier, inc=1, device_id={axis: index}, device_id_type=MESH)

    greet("gx", partner)
    pl.when(has_out)(lambda: greet("gx", outward))
    pl.when(has_in)(lambda: greet("gx", inward))
    pl.when(has_low)(lambda: greet("gy", iy - 1))
    pl.when(has_high)(lambda: greet("gy", iy + 1))

    for wide in wides:
        for field in range(2):

            @pl.when(jnp.logical_not(has_in))
            def _():
                wide[field, core, near_at, :] = jnp.zeros((cells_y, cells_x, LANES), jnp.float32)

            @pl.when(jnp.logical_not(has_out))
            def _():
                wide[field, core, far_at, :] = jnp.zeros((cells_y, cells_x, LANES), jnp.float32)

            edge = jnp.zeros((RADIUS, 4 * cells_x, LANES), jnp.float32)

            @pl.when(jnp.logical_not(has_low))
            def _():
                wide[field, pl.ds(0, RADIUS)] = edge

            @pl.when(jnp.logical_not(has_high))
            def _():
                wide[field, pl.ds(cells_y + RADIUS, RADIUS)] = edge

    pl.semaphore_wait(
        barrier,
        1 + sum(flag.astype(jnp.int32) for flag in (has_out, has_in, has_low, has_high)),
    )

    def remote(pair, kind, src, dst, axis, index):
        return pltpu.make_async_remote_copy(
            src_ref=src,
            dst_ref=dst,
            send_sem=send_sem.at[pair, kind],
            recv_sem=recv_sem.at[pair, kind],
            device_id={axis: index},
            device_id_type=MESH,
        )

    def swap_copy(pair):
        dst = wides[pair].at[:, core, own_at, :]
        return remote(pair, SWAP, sent.at[pair], dst, "gx", partner)

    def swap_arrival(pair):
        dst = wides[pair].at[:, core, recv_at, :]
        return remote(pair, SWAP, sent.at[pair], dst, "gx", partner)

    def near_copy(pair):
        return remote(
            pair, NEAR, own.at[pair], wides[pair].at[:, core, near_at, :], "gx", outward
        )

    def far_copy(pair):
        wide = wides[pair]
        return remote(
            pair,
            FAR,
            wide.at[:, core, recv_at, :],
            wide.at[:, core, far_at, :],
            "gx",
            inward,
        )

    def edge_copies(pair, kind, at):
        wide = wides[pair]
        size = RADIUS
        up = remote(
            pair,
            kind,
            wide.at[:, pl.ds(cells_y, size), at, :],
            wide.at[:, pl.ds(0, size), at, :],
            "gy",
            iy + 1,
        )
        down = remote(
            pair,
            kind + 1,
            wide.at[:, pl.ds(RADIUS, size), at, :],
            wide.at[:, pl.ds(cells_y + RADIUS, size), at, :],
            "gy",
            iy - 1,
        )
        return up, down

    def start_edges(pair, kind, at):
        up, down = edge_copies(pair, kind, at)
        pl.when(has_high)(up.start)
        pl.when(has_low)(down.start)

    def wait_edges(pair, kind, at):
        up, down = edge_copies(pair, kind, at)
        pl.when(has_low)(up.wait_recv)
        pl.when(has_high)(down.wait_recv)

    def own_copy(pair):
        return pltpu.make_async_copy(
            own.at[pair], wides[pair].at[:, core, own_at, :], own_sem.at[pair]
        )

    def out_copy(pair, field):
        return remote(
            pair,
            OUT + field,
            stages[pair].at[1, field],
            outs[field].at[pair, :, lane_at],
            "gx",
            partner,
        )

    def out_arrival(pair, field):
        theirs = pl.ds(pl.multiple_of((1 - parity) * LANES, LANES), LANES)
        return remote(
            pair,
            OUT + field,
            stages[pair].at[1, field],
            outs[field].at[pair, :, theirs],
            "gx",
            partner,
        )

    def mine_copy(pair, field):
        return pltpu.make_async_copy(
            stages[pair].at[0, field],
            outs[field].at[pair, :, lane_at],
            mine_sem.at[pair, field],
        )

    def compute(pair, side):
        wide, stage = wides[pair], stages[pair]
        rows = cells_y + 2 * RADIUS
        row = rows_of[pair]
        upper = side + parity - 2 * side * parity

        @pl.loop(0, 2 * blocks)
        def _(step):
            field = step // blocks
            block = step - field * blocks
            sign = 2 - 4 * field
            base = cells_x + upper * cells_x + block * SUB
            at = pl.ds(pl.multiple_of(base, SUB), SUB)
            centre = [wide[field, y, at, :] for y in range(rows)]

            def term(h, totals):
                moved = pl.ds(base + sign * lags[h], SUB)
                weight = weights[row, h] * 0.0625
                other = [wide[1 - field, y, moved, :] for y in range(rows)]
                image = smooth_rows([c * o for c, o in zip(centre, other)])
                return tuple(
                    total + (weight * value) * o
                    for total, value, o in zip(totals, image, other[RADIUS:])
                )

            zeros = tuple(jnp.zeros((SUB, LANES), jnp.float32) for _ in range(cells_y))
            totals = lax.fori_loop(0, noff, term, zeros)
            first = block * SUB * cells_y
            for y in range(cells_y):
                stage[side, field, pl.ds(first + y, SUB, stride=cells_y), :] = totals[y]

    pairs = range(pair_count)
    for pair in pairs:
        swap_copy(pair).start()
        pl.when(has_out)(near_copy(pair).start)
    for pair in pairs:
        own_copy(pair).start()
    for pair in pairs:
        own_copy(pair).wait()

    def forward(pair):
        swap_arrival(pair).wait_recv()
        pl.when(has_in)(far_copy(pair).start)
        pl.when(has_in)(near_copy(pair).wait_recv)
        start_edges(pair, REST_UP, rest_at)

    def finish(pair):
        pl.when(has_out)(far_copy(pair).wait_recv)
        start_edges(pair, FAR_UP, far_at)

    def settle(pair):
        wait_edges(pair, REST_UP, rest_at)
        wait_edges(pair, FAR_UP, far_at)

    forward(0)
    for pair in pairs:
        if pair + 1 < pair_count:
            forward(pair + 1)
        finish(pair)
        settle(pair)
        compute(pair, 1)
        for field in range(2):
            out_copy(pair, field).start()
        compute(pair, 0)
        for field in range(2):
            mine_copy(pair, field).start()

    for pair in pairs:
        swap_copy(pair).wait_send()
        pl.when(has_out)(near_copy(pair).wait_send)
        pl.when(has_in)(far_copy(pair).wait_send)
        for kind, at in ((REST_UP, rest_at), (FAR_UP, far_at)):
            up, down = edge_copies(pair, kind, at)
            pl.when(has_high)(up.wait_send)
            pl.when(has_low)(down.wait_send)
        for field in range(2):
            mine_copy(pair, field).wait()
            out_copy(pair, field).wait_send()
            out_arrival(pair, field).wait_recv()


def local(source_snaps, receiver_snaps, snap_pairs, offset_lags, weight_table, weight_index):
    _, cells_x, cells_y, depth = source_snaps.shape
    pair_count = snap_pairs.shape[0]
    own, sent = gather(snap_pairs, source_snaps, receiver_snaps)
    smem = pl.BlockSpec(memory_space=pltpu.SMEM)
    anywhere = pl.BlockSpec(memory_space=pl.ANY)
    wide = pltpu.VMEM((2, cells_y + 2 * RADIUS, 4 * cells_x, LANES), jnp.float32)
    stage = pltpu.VMEM((2, 2, cells_x * cells_y, LANES), jnp.float32)
    out = pl.pallas_call(
        functools.partial(adjoint_kernel, lax.axis_size("gx"), lax.axis_size("gy")),
        out_shape=[
            jax.ShapeDtypeStruct((pair_count, cells_x * cells_y, depth), jnp.float32)
        ] * 2,
        in_specs=[smem] * 3 + [pl.BlockSpec(memory_space=pltpu.HBM)] * 2,
        out_specs=[anywhere] * 2,
        scratch_shapes=[wide] * pair_count
        + [stage] * pair_count
        + [
            pltpu.SemaphoreType.DMA((pair_count, KINDS)),
            pltpu.SemaphoreType.DMA((pair_count, KINDS)),
            pltpu.SemaphoreType.DMA((pair_count,)),
            pltpu.SemaphoreType.DMA((pair_count, 2)),
        ],
        compiler_params=pltpu.CompilerParams(
            collective_id=0, has_side_effects=True, vmem_limit_bytes=48 * 1024 * 1024
        ),
        name="adjoints",
    )(offset_lags, weight_table, weight_index, own, sent)
    return tuple(a.reshape(pair_count, cells_x, cells_y, depth) for a in out)


def solution(mesh):
    return jax.shard_map(
        local,
        mesh=mesh,
        in_specs=(P(None, "gx", "gy", None), P(None, "gx", "gy", None), P(), P(), P(), P()),
        out_specs=(P(None, "gx", "gy", None), P(None, "gx", "gy", None)),
        check_vma=False,
    )
```

```python
import functools

import jax
import jax.numpy as jnp
from jax import lax
from jax.experimental import pallas as pl
from jax.experimental.pallas import tpu as pltpu
from jax.sharding import PartitionSpec as P

SUB = 8
LANES = 128
RADIUS = 2
MESH = pl.DeviceIdType.MESH
SWAP, NEAR, FAR, REST_UP, REST_DOWN, FAR_UP, FAR_DOWN, OUT = range(8)
KINDS = OUT + 2


def smooth_rows(rows):
    for _ in range(2 * RADIUS):
        rows = [low + high for low, high in zip(rows[:-1], rows[1:])]
    return rows


def gather_kernel(pairs, source, receiver, own, sent):
    parity = lax.rem(lax.axis_index("gx"), 2)
    for field, ref in enumerate((source, receiver)):
        for out, side in ((own, parity), (sent, 1 - parity)):
            at = pl.ds(pl.multiple_of(side * LANES, LANES), LANES)
            out[0, field] = jnp.swapaxes(ref[0, :, :, at], 0, 1)


def gather(snap_pairs, source_snaps, receiver_snaps):
    _, cells_x, cells_y, depth = source_snaps.shape
    pair_count = snap_pairs.shape[0]
    block = (1, cells_x, SUB, depth)
    shape = (2, cells_y, cells_x, LANES)
    out = pl.BlockSpec((1, 2, SUB, cells_x, LANES), lambda p, y, pairs: (p, 0, y, 0, 0))
    return pl.pallas_call(
        gather_kernel,
        out_shape=[jax.ShapeDtypeStruct((pair_count, *shape), jnp.float32)] * 2,
        grid_spec=pltpu.PrefetchScalarGridSpec(
            num_scalar_prefetch=1,
            grid=(pair_count, cells_y // SUB),
            in_specs=[
                pl.BlockSpec(block, lambda p, y, pairs: (pairs[0, p], 0, y, 0)),
                pl.BlockSpec(block, lambda p, y, pairs: (pairs[1, p], 0, y, 0)),
            ],
            out_specs=[out, out],
        ),
        compiler_params=pltpu.CompilerParams(vmem_limit_bytes=58 * 1024 * 1024),
        name="gather",
    )(snap_pairs.T, source_snaps, receiver_snaps)


def adjoint_kernel(
    gx, gy, lags, weights, rows_of, own, sent, out_s, out_r, *scratch
):
    pair_count = own.shape[0]
    cells_y, cells_x = own.shape[2:4]
    wides = scratch[:pair_count]
    stages = scratch[pair_count : 2 * pair_count]
    send_sem, recv_sem, own_sem, mine_sem = scratch[2 * pair_count :]
    outs = (out_s, out_r)
    noff = lags.shape[0]
    blocks = cells_x // SUB

    ix = lax.axis_index("gx")
    iy = lax.axis_index("gy")
    parity = lax.rem(ix, 2)
    partner = ix + 1 - 2 * parity
    outward = ix - 2 + 4 * parity
    inward = ix + 2 - 4 * parity
    has_out = (outward >= 0) & (outward < gx)
    has_in = (inward >= 0) & (inward < gx)
    has_low = iy > 0
    has_high = iy < gy - 1

    own_at = pl.ds(pl.multiple_of(cells_x + cells_x * parity, SUB), cells_x)
    recv_at = pl.ds(pl.multiple_of(2 * cells_x - cells_x * parity, SUB), cells_x)
    near_at = pl.ds(pl.multiple_of(3 * cells_x - 3 * cells_x * parity, SUB), cells_x)
    far_at = pl.ds(pl.multiple_of(3 * cells_x * parity, SUB), cells_x)
    rest_at = pl.ds(pl.multiple_of(cells_x - cells_x * parity, SUB), 3 * cells_x)
    core = pl.ds(RADIUS, cells_y)
    lane_at = pl.ds(pl.multiple_of(parity * LANES, LANES), LANES)

    barrier = pltpu.get_barrier_semaphore()

    def greet(axis, index):
        pl.semaphore_signal(barrier, inc=1, device_id={axis: index}, device_id_type=MESH)

    greet("gx", partner)
    pl.when(has_out)(lambda: greet("gx", outward))
    pl.when(has_in)(lambda: greet("gx", inward))
    pl.when(has_low)(lambda: greet("gy", iy - 1))
    pl.when(has_high)(lambda: greet("gy", iy + 1))

    for wide in wides:
        for field in range(2):

            @pl.when(jnp.logical_not(has_in))
            def _():
                wide[field, core, near_at, :] = jnp.zeros((cells_y, cells_x, LANES), jnp.float32)

            @pl.when(jnp.logical_not(has_out))
            def _():
                wide[field, core, far_at, :] = jnp.zeros((cells_y, cells_x, LANES), jnp.float32)

            edge = jnp.zeros((RADIUS, 4 * cells_x, LANES), jnp.float32)

            @pl.when(jnp.logical_not(has_low))
            def _():
                wide[field, pl.ds(0, RADIUS)] = edge

            @pl.when(jnp.logical_not(has_high))
            def _():
                wide[field, pl.ds(cells_y + RADIUS, RADIUS)] = edge

    pl.semaphore_wait(
        barrier,
        1 + sum(flag.astype(jnp.int32) for flag in (has_out, has_in, has_low, has_high)),
    )

    def remote(pair, kind, src, dst, axis, index):
        return pltpu.make_async_remote_copy(
            src_ref=src,
            dst_ref=dst,
            send_sem=send_sem.at[pair, kind],
            recv_sem=recv_sem.at[pair, kind],
            device_id={axis: index},
            device_id_type=MESH,
        )

    def swap_copy(pair):
        dst = wides[pair].at[:, core, own_at, :]
        return remote(pair, SWAP, sent.at[pair], dst, "gx", partner)

    def swap_arrival(pair):
        dst = wides[pair].at[:, core, recv_at, :]
        return remote(pair, SWAP, sent.at[pair], dst, "gx", partner)

    def near_copy(pair):
        return remote(
            pair, NEAR, own.at[pair], wides[pair].at[:, core, near_at, :], "gx", outward
        )

    def far_copy(pair):
        wide = wides[pair]
        return remote(
            pair,
            FAR,
            wide.at[:, core, recv_at, :],
            wide.at[:, core, far_at, :],
            "gx",
            inward,
        )

    def edge_copies(pair, kind, at):
        wide = wides[pair]
        size = RADIUS
        up = remote(
            pair,
            kind,
            wide.at[:, pl.ds(cells_y, size), at, :],
            wide.at[:, pl.ds(0, size), at, :],
            "gy",
            iy + 1,
        )
        down = remote(
            pair,
            kind + 1,
            wide.at[:, pl.ds(RADIUS, size), at, :],
            wide.at[:, pl.ds(cells_y + RADIUS, size), at, :],
            "gy",
            iy - 1,
        )
        return up, down

    def start_edges(pair, kind, at):
        up, down = edge_copies(pair, kind, at)
        pl.when(has_high)(up.start)
        pl.when(has_low)(down.start)

    def wait_edges(pair, kind, at):
        up, down = edge_copies(pair, kind, at)
        pl.when(has_low)(up.wait_recv)
        pl.when(has_high)(down.wait_recv)

    def own_copy(pair):
        return pltpu.make_async_copy(
            own.at[pair], wides[pair].at[:, core, own_at, :], own_sem.at[pair]
        )

    def out_copy(pair, field):
        return remote(
            pair,
            OUT + field,
            stages[pair].at[1, field],
            outs[field].at[pair, :, lane_at],
            "gx",
            partner,
        )

    def out_arrival(pair, field):
        theirs = pl.ds(pl.multiple_of((1 - parity) * LANES, LANES), LANES)
        return remote(
            pair,
            OUT + field,
            stages[pair].at[1, field],
            outs[field].at[pair, :, theirs],
            "gx",
            partner,
        )

    def mine_copy(pair, field):
        return pltpu.make_async_copy(
            stages[pair].at[0, field],
            outs[field].at[pair, :, lane_at],
            mine_sem.at[pair, field],
        )

    def compute(pair, side, field):
        wide, stage = wides[pair], stages[pair]
        rows = cells_y + 2 * RADIUS
        row = rows_of[pair]
        upper = side + parity - 2 * side * parity

        sign = 2 - 4 * field

        @pl.loop(0, blocks)
        def _(block):
            base = cells_x + upper * cells_x + block * SUB
            at = pl.ds(pl.multiple_of(base, SUB), SUB)
            centre = [wide[field, y, at, :] for y in range(rows)]

            def term(h, totals):
                moved = pl.ds(base + sign * lags[h], SUB)
                weight = weights[row, h] * 0.0625
                other = [wide[1 - field, y, moved, :] for y in range(rows)]
                image = smooth_rows([c * o for c, o in zip(centre, other)])
                return tuple(
                    total + (weight * value) * o
                    for total, value, o in zip(totals, image, other[RADIUS:])
                )

            zeros = tuple(jnp.zeros((SUB, LANES), jnp.float32) for _ in range(cells_y))
            totals = lax.fori_loop(0, noff, term, zeros)
            first = block * SUB * cells_y
            for y in range(cells_y):
                stage[side, field, pl.ds(first + y, SUB, stride=cells_y), :] = totals[y]

    pairs = range(pair_count)
    for pair in pairs:
        swap_copy(pair).start()
        pl.when(has_out)(near_copy(pair).start)
    for pair in pairs:
        own_copy(pair).start()
    for pair in pairs:
        own_copy(pair).wait()

    def forward(pair):
        swap_arrival(pair).wait_recv()
        pl.when(has_in)(far_copy(pair).start)
        pl.when(has_in)(near_copy(pair).wait_recv)
        start_edges(pair, REST_UP, rest_at)

    def finish(pair):
        pl.when(has_out)(far_copy(pair).wait_recv)
        start_edges(pair, FAR_UP, far_at)

    def settle(pair):
        wait_edges(pair, REST_UP, rest_at)
        wait_edges(pair, FAR_UP, far_at)

    forward(0)
    for pair in pairs:
        if pair + 1 < pair_count:
            forward(pair + 1)
        finish(pair)
        settle(pair)
        for field in range(2):
            compute(pair, 1, field)
            out_copy(pair, field).start()
        for field in range(2):
            compute(pair, 0, field)
            mine_copy(pair, field).start()

    for pair in pairs:
        swap_copy(pair).wait_send()
        pl.when(has_out)(near_copy(pair).wait_send)
        pl.when(has_in)(far_copy(pair).wait_send)
        for kind, at in ((REST_UP, rest_at), (FAR_UP, far_at)):
            up, down = edge_copies(pair, kind, at)
            pl.when(has_high)(up.wait_send)
            pl.when(has_low)(down.wait_send)
        for field in range(2):
            mine_copy(pair, field).wait()
            out_copy(pair, field).wait_send()
            out_arrival(pair, field).wait_recv()


def local(source_snaps, receiver_snaps, snap_pairs, offset_lags, weight_table, weight_index):
    _, cells_x, cells_y, depth = source_snaps.shape
    pair_count = snap_pairs.shape[0]
    own, sent = gather(snap_pairs, source_snaps, receiver_snaps)
    smem = pl.BlockSpec(memory_space=pltpu.SMEM)
    anywhere = pl.BlockSpec(memory_space=pl.ANY)
    wide = pltpu.VMEM((2, cells_y + 2 * RADIUS, 4 * cells_x, LANES), jnp.float32)
    stage = pltpu.VMEM((2, 2, cells_x * cells_y, LANES), jnp.float32)
    out = pl.pallas_call(
        functools.partial(adjoint_kernel, lax.axis_size("gx"), lax.axis_size("gy")),
        out_shape=[
            jax.ShapeDtypeStruct((pair_count, cells_x * cells_y, depth), jnp.float32)
        ] * 2,
        in_specs=[smem] * 3 + [pl.BlockSpec(memory_space=pltpu.HBM)] * 2,
        out_specs=[anywhere] * 2,
        scratch_shapes=[wide] * pair_count
        + [stage] * pair_count
        + [
            pltpu.SemaphoreType.DMA((pair_count, KINDS)),
            pltpu.SemaphoreType.DMA((pair_count, KINDS)),
            pltpu.SemaphoreType.DMA((pair_count,)),
            pltpu.SemaphoreType.DMA((pair_count, 2)),
        ],
        compiler_params=pltpu.CompilerParams(
            collective_id=0, has_side_effects=True, vmem_limit_bytes=48 * 1024 * 1024
        ),
        name="adjoints",
    )(offset_lags, weight_table, weight_index, own, sent)
    return tuple(a.reshape(pair_count, cells_x, cells_y, depth) for a in out)


def solution(mesh):
    return jax.shard_map(
        local,
        mesh=mesh,
        in_specs=(P(None, "gx", "gy", None), P(None, "gx", "gy", None), P(), P(), P(), P()),
        out_specs=(P(None, "gx", "gy", None), P(None, "gx", "gy", None)),
        check_vma=False,
    )
```

```python
import functools

import jax
import jax.numpy as jnp
from jax import lax
from jax.experimental import pallas as pl
from jax.experimental.pallas import tpu as pltpu
from jax.sharding import PartitionSpec as P

SUB = 8
LANES = 128
RADIUS = 2
MESH = pl.DeviceIdType.MESH
SWAP, NEAR, FAR, REST_UP, REST_DOWN, FAR_UP, FAR_DOWN, OUT = range(8)
KINDS = OUT + 2


def smooth_rows(rows):
    for _ in range(2 * RADIUS):
        rows = [low + high for low, high in zip(rows[:-1], rows[1:])]
    return rows


def gather_kernel(pairs, source, receiver, own, sent, held, turned, in_sem, out_sem):
    parity = lax.rem(lax.axis_index("gx"), 2)
    pair_count = own.shape[0]

    def read(pair, field):
        ref = (source, receiver)[field]
        return pltpu.make_async_copy(
            ref.at[pairs[field, pair]], held.at[pair, field], in_sem.at[pair, field]
        )

    def write(pair, which):
        out = (own, sent)[which]
        return pltpu.make_async_copy(
            turned.at[pair, which], out.at[pair], out_sem.at[pair, which]
        )

    for pair in range(pair_count):
        for field in range(2):
            read(pair, field).start()
    for pair in range(pair_count):
        for field in range(2):
            read(pair, field).wait()
            for which, side in enumerate((parity, 1 - parity)):
                at = pl.ds(pl.multiple_of(side * LANES, LANES), LANES)
                turned[pair, which, field] = jnp.swapaxes(held[pair, field, :, :, at], 0, 1)
        for which in range(2):
            write(pair, which).start()
    for pair in range(pair_count):
        for which in range(2):
            write(pair, which).wait()


def gather(snap_pairs, source_snaps, receiver_snaps):
    _, cells_x, cells_y, depth = source_snaps.shape
    pair_count = snap_pairs.shape[0]
    shape = (2, cells_y, cells_x, LANES)
    anywhere = pl.BlockSpec(memory_space=pl.ANY)
    return pl.pallas_call(
        gather_kernel,
        out_shape=[jax.ShapeDtypeStruct((pair_count, *shape), jnp.float32)] * 2,
        in_specs=[pl.BlockSpec(memory_space=pltpu.SMEM), anywhere, anywhere],
        out_specs=[anywhere, anywhere],
        scratch_shapes=[
            pltpu.VMEM((pair_count, 2, cells_x, cells_y, depth), jnp.float32),
            pltpu.VMEM((pair_count, 2, *shape), jnp.float32),
            pltpu.SemaphoreType.DMA((pair_count, 2)),
            pltpu.SemaphoreType.DMA((pair_count, 2)),
        ],
        compiler_params=pltpu.CompilerParams(vmem_limit_bytes=58 * 1024 * 1024),
        name="gather",
    )(snap_pairs.T, source_snaps, receiver_snaps)


def adjoint_kernel(
    gx, gy, lags, weights, rows_of, own, sent, out_s, out_r, *scratch
):
    pair_count = own.shape[0]
    cells_y, cells_x = own.shape[2:4]
    wides = scratch[:pair_count]
    stages = scratch[pair_count : 2 * pair_count]
    send_sem, recv_sem, own_sem, mine_sem = scratch[2 * pair_count :]
    outs = (out_s, out_r)
    noff = lags.shape[0]
    blocks = cells_x // SUB

    ix = lax.axis_index("gx")
    iy = lax.axis_index("gy")
    parity = lax.rem(ix, 2)
    partner = ix + 1 - 2 * parity
    outward = ix - 2 + 4 * parity
    inward = ix + 2 - 4 * parity
    has_out = (outward >= 0) & (outward < gx)
    has_in = (inward >= 0) & (inward < gx)
    has_low = iy > 0
    has_high = iy < gy - 1

    own_at = pl.ds(pl.multiple_of(cells_x + cells_x * parity, SUB), cells_x)
    recv_at = pl.ds(pl.multiple_of(2 * cells_x - cells_x * parity, SUB), cells_x)
    near_at = pl.ds(pl.multiple_of(3 * cells_x - 3 * cells_x * parity, SUB), cells_x)
    far_at = pl.ds(pl.multiple_of(3 * cells_x * parity, SUB), cells_x)
    rest_at = pl.ds(pl.multiple_of(cells_x - cells_x * parity, SUB), 3 * cells_x)
    core = pl.ds(RADIUS, cells_y)
    lane_at = pl.ds(pl.multiple_of(parity * LANES, LANES), LANES)

    barrier = pltpu.get_barrier_semaphore()

    def greet(axis, index):
        pl.semaphore_signal(barrier, inc=1, device_id={axis: index}, device_id_type=MESH)

    greet("gx", partner)
    pl.when(has_out)(lambda: greet("gx", outward))
    pl.when(has_in)(lambda: greet("gx", inward))
    pl.when(has_low)(lambda: greet("gy", iy - 1))
    pl.when(has_high)(lambda: greet("gy", iy + 1))

    for wide in wides:
        for field in range(2):

            @pl.when(jnp.logical_not(has_in))
            def _():
                wide[field, core, near_at, :] = jnp.zeros((cells_y, cells_x, LANES), jnp.float32)

            @pl.when(jnp.logical_not(has_out))
            def _():
                wide[field, core, far_at, :] = jnp.zeros((cells_y, cells_x, LANES), jnp.float32)

            edge = jnp.zeros((RADIUS, 4 * cells_x, LANES), jnp.float32)

            @pl.when(jnp.logical_not(has_low))
            def _():
                wide[field, pl.ds(0, RADIUS)] = edge

            @pl.when(jnp.logical_not(has_high))
            def _():
                wide[field, pl.ds(cells_y + RADIUS, RADIUS)] = edge

    pl.semaphore_wait(
        barrier,
        1 + sum(flag.astype(jnp.int32) for flag in (has_out, has_in, has_low, has_high)),
    )

    def remote(pair, kind, src, dst, axis, index):
        return pltpu.make_async_remote_copy(
            src_ref=src,
            dst_ref=dst,
            send_sem=send_sem.at[pair, kind],
            recv_sem=recv_sem.at[pair, kind],
            device_id={axis: index},
            device_id_type=MESH,
        )

    def swap_copy(pair):
        dst = wides[pair].at[:, core, own_at, :]
        return remote(pair, SWAP, sent.at[pair], dst, "gx", partner)

    def swap_arrival(pair):
        dst = wides[pair].at[:, core, recv_at, :]
        return remote(pair, SWAP, sent.at[pair], dst, "gx", partner)

    def near_copy(pair):
        return remote(
            pair, NEAR, own.at[pair], wides[pair].at[:, core, near_at, :], "gx", outward
        )

    def far_copy(pair):
        wide = wides[pair]
        return remote(
            pair,
            FAR,
            wide.at[:, core, recv_at, :],
            wide.at[:, core, far_at, :],
            "gx",
            inward,
        )

    def edge_copies(pair, kind, at):
        wide = wides[pair]
        size = RADIUS
        up = remote(
            pair,
            kind,
            wide.at[:, pl.ds(cells_y, size), at, :],
            wide.at[:, pl.ds(0, size), at, :],
            "gy",
            iy + 1,
        )
        down = remote(
            pair,
            kind + 1,
            wide.at[:, pl.ds(RADIUS, size), at, :],
            wide.at[:, pl.ds(cells_y + RADIUS, size), at, :],
            "gy",
            iy - 1,
        )
        return up, down

    def start_edges(pair, kind, at):
        up, down = edge_copies(pair, kind, at)
        pl.when(has_high)(up.start)
        pl.when(has_low)(down.start)

    def wait_edges(pair, kind, at):
        up, down = edge_copies(pair, kind, at)
        pl.when(has_low)(up.wait_recv)
        pl.when(has_high)(down.wait_recv)

    def own_copy(pair):
        return pltpu.make_async_copy(
            own.at[pair], wides[pair].at[:, core, own_at, :], own_sem.at[pair]
        )

    def out_copy(pair, field):
        return remote(
            pair,
            OUT + field,
            stages[pair].at[1, field],
            outs[field].at[pair, :, lane_at],
            "gx",
            partner,
        )

    def out_arrival(pair, field):
        theirs = pl.ds(pl.multiple_of((1 - parity) * LANES, LANES), LANES)
        return remote(
            pair,
            OUT + field,
            stages[pair].at[1, field],
            outs[field].at[pair, :, theirs],
            "gx",
            partner,
        )

    def mine_copy(pair, field):
        return pltpu.make_async_copy(
            stages[pair].at[0, field],
            outs[field].at[pair, :, lane_at],
            mine_sem.at[pair, field],
        )

    def compute(pair, side, field):
        wide, stage = wides[pair], stages[pair]
        rows = cells_y + 2 * RADIUS
        row = rows_of[pair]
        upper = side + parity - 2 * side * parity

        sign = 2 - 4 * field

        @pl.loop(0, blocks)
        def _(block):
            base = cells_x + upper * cells_x + block * SUB
            at = pl.ds(pl.multiple_of(base, SUB), SUB)
            centre = [wide[field, y, at, :] for y in range(rows)]

            def term(h, totals):
                moved = pl.ds(base + sign * lags[h], SUB)
                weight = weights[row, h] * 0.0625
                other = [wide[1 - field, y, moved, :] for y in range(rows)]
                image = smooth_rows([c * o for c, o in zip(centre, other)])
                return tuple(
                    total + (weight * value) * o
                    for total, value, o in zip(totals, image, other[RADIUS:])
                )

            zeros = tuple(jnp.zeros((SUB, LANES), jnp.float32) for _ in range(cells_y))
            totals = lax.fori_loop(0, noff, term, zeros)
            first = block * SUB * cells_y
            for y in range(cells_y):
                stage[side, field, pl.ds(first + y, SUB, stride=cells_y), :] = totals[y]

    pairs = range(pair_count)
    for pair in pairs:
        swap_copy(pair).start()
        pl.when(has_out)(near_copy(pair).start)
    for pair in pairs:
        own_copy(pair).start()
    for pair in pairs:
        own_copy(pair).wait()

    def forward(pair):
        swap_arrival(pair).wait_recv()
        pl.when(has_in)(far_copy(pair).start)
        pl.when(has_in)(near_copy(pair).wait_recv)
        start_edges(pair, REST_UP, rest_at)

    def finish(pair):
        pl.when(has_out)(far_copy(pair).wait_recv)
        start_edges(pair, FAR_UP, far_at)

    def settle(pair):
        wait_edges(pair, REST_UP, rest_at)
        wait_edges(pair, FAR_UP, far_at)

    forward(0)
    for pair in pairs:
        if pair + 1 < pair_count:
            forward(pair + 1)
        finish(pair)
        settle(pair)
        for field in range(2):
            compute(pair, 1, field)
            out_copy(pair, field).start()
        for field in range(2):
            compute(pair, 0, field)
            mine_copy(pair, field).start()

    for pair in pairs:
        swap_copy(pair).wait_send()
        pl.when(has_out)(near_copy(pair).wait_send)
        pl.when(has_in)(far_copy(pair).wait_send)
        for kind, at in ((REST_UP, rest_at), (FAR_UP, far_at)):
            up, down = edge_copies(pair, kind, at)
            pl.when(has_high)(up.wait_send)
            pl.when(has_low)(down.wait_send)
        for field in range(2):
            mine_copy(pair, field).wait()
            out_copy(pair, field).wait_send()
            out_arrival(pair, field).wait_recv()


def local(source_snaps, receiver_snaps, snap_pairs, offset_lags, weight_table, weight_index):
    _, cells_x, cells_y, depth = source_snaps.shape
    pair_count = snap_pairs.shape[0]
    own, sent = gather(snap_pairs, source_snaps, receiver_snaps)
    smem = pl.BlockSpec(memory_space=pltpu.SMEM)
    anywhere = pl.BlockSpec(memory_space=pl.ANY)
    wide = pltpu.VMEM((2, cells_y + 2 * RADIUS, 4 * cells_x, LANES), jnp.float32)
    stage = pltpu.VMEM((2, 2, cells_x * cells_y, LANES), jnp.float32)
    out = pl.pallas_call(
        functools.partial(adjoint_kernel, lax.axis_size("gx"), lax.axis_size("gy")),
        out_shape=[
            jax.ShapeDtypeStruct((pair_count, cells_x * cells_y, depth), jnp.float32)
        ] * 2,
        in_specs=[smem] * 3 + [pl.BlockSpec(memory_space=pltpu.HBM)] * 2,
        out_specs=[anywhere] * 2,
        scratch_shapes=[wide] * pair_count
        + [stage] * pair_count
        + [
            pltpu.SemaphoreType.DMA((pair_count, KINDS)),
            pltpu.SemaphoreType.DMA((pair_count, KINDS)),
            pltpu.SemaphoreType.DMA((pair_count,)),
            pltpu.SemaphoreType.DMA((pair_count, 2)),
        ],
        compiler_params=pltpu.CompilerParams(
            collective_id=0, has_side_effects=True, vmem_limit_bytes=48 * 1024 * 1024
        ),
        name="adjoints",
    )(offset_lags, weight_table, weight_index, own, sent)
    return tuple(a.reshape(pair_count, cells_x, cells_y, depth) for a in out)


def solution(mesh):
    return jax.shard_map(
        local,
        mesh=mesh,
        in_specs=(P(None, "gx", "gy", None), P(None, "gx", "gy", None), P(), P(), P(), P()),
        out_specs=(P(None, "gx", "gy", None), P(None, "gx", "gy", None)),
        check_vma=False,
    )
```

```python
import functools

import jax
import jax.numpy as jnp
from jax import lax
from jax.experimental import pallas as pl
from jax.experimental.pallas import tpu as pltpu
from jax.sharding import PartitionSpec as P

SUB = 8
LANES = 128
RADIUS = 2
MESH = pl.DeviceIdType.MESH
SWAP, NEAR, FAR, REST_UP, REST_DOWN, FAR_UP, FAR_DOWN, OUT = range(8)
KINDS = OUT + 2


def smooth_rows(rows):
    for _ in range(2 * RADIUS):
        rows = [low + high for low, high in zip(rows[:-1], rows[1:])]
    return rows


def gather_kernel(pairs, source, receiver, own, sent, held, turned, in_sem, out_sem):
    parity = lax.rem(lax.axis_index("gx"), 2)
    pair_count = own.shape[0]

    def read(pair, field):
        ref = (source, receiver)[field]
        return pltpu.make_async_copy(
            ref.at[pairs[field, pair]], held.at[pair, field], in_sem.at[pair, field]
        )

    def write(pair, which, field):
        out = (own, sent)[which]
        return pltpu.make_async_copy(
            turned.at[pair, which, field], out.at[pair, field], out_sem.at[pair, which, field]
        )

    for pair in range(pair_count):
        for field in range(2):
            read(pair, field).start()
    for pair in range(pair_count):
        for field in range(2):
            read(pair, field).wait()
            for which, side in enumerate((parity, 1 - parity)):
                at = pl.ds(pl.multiple_of(side * LANES, LANES), LANES)
                turned[pair, which, field] = jnp.swapaxes(held[pair, field, :, :, at], 0, 1)
                write(pair, which, field).start()
    for pair in range(pair_count):
        for field in range(2):
            for which in range(2):
                write(pair, which, field).wait()


def gather(snap_pairs, source_snaps, receiver_snaps):
    _, cells_x, cells_y, depth = source_snaps.shape
    pair_count = snap_pairs.shape[0]
    shape = (2, cells_y, cells_x, LANES)
    anywhere = pl.BlockSpec(memory_space=pl.ANY)
    return pl.pallas_call(
        gather_kernel,
        out_shape=[jax.ShapeDtypeStruct((pair_count, *shape), jnp.float32)] * 2,
        in_specs=[pl.BlockSpec(memory_space=pltpu.SMEM), anywhere, anywhere],
        out_specs=[anywhere, anywhere],
        scratch_shapes=[
            pltpu.VMEM((pair_count, 2, cells_x, cells_y, depth), jnp.float32),
            pltpu.VMEM((pair_count, 2, *shape), jnp.float32),
            pltpu.SemaphoreType.DMA((pair_count, 2)),
            pltpu.SemaphoreType.DMA((pair_count, 2, 2)),
        ],
        compiler_params=pltpu.CompilerParams(vmem_limit_bytes=58 * 1024 * 1024),
        name="gather",
    )(snap_pairs.T, source_snaps, receiver_snaps)


def adjoint_kernel(
    gx, gy, lags, weights, rows_of, own, sent, out_s, out_r, *scratch
):
    pair_count = own.shape[0]
    cells_y, cells_x = own.shape[2:4]
    wides = scratch[:pair_count]
    stages = scratch[pair_count : 2 * pair_count]
    send_sem, recv_sem, own_sem, mine_sem = scratch[2 * pair_count :]
    outs = (out_s, out_r)
    noff = lags.shape[0]
    blocks = cells_x // SUB

    ix = lax.axis_index("gx")
    iy = lax.axis_index("gy")
    parity = lax.rem(ix, 2)
    partner = ix + 1 - 2 * parity
    outward = ix - 2 + 4 * parity
    inward = ix + 2 - 4 * parity
    has_out = (outward >= 0) & (outward < gx)
    has_in = (inward >= 0) & (inward < gx)
    has_low = iy > 0
    has_high = iy < gy - 1

    own_at = pl.ds(pl.multiple_of(cells_x + cells_x * parity, SUB), cells_x)
    recv_at = pl.ds(pl.multiple_of(2 * cells_x - cells_x * parity, SUB), cells_x)
    near_at = pl.ds(pl.multiple_of(3 * cells_x - 3 * cells_x * parity, SUB), cells_x)
    far_at = pl.ds(pl.multiple_of(3 * cells_x * parity, SUB), cells_x)
    rest_at = pl.ds(pl.multiple_of(cells_x - cells_x * parity, SUB), 3 * cells_x)
    core = pl.ds(RADIUS, cells_y)
    lane_at = pl.ds(pl.multiple_of(parity * LANES, LANES), LANES)

    barrier = pltpu.get_barrier_semaphore()

    def greet(axis, index):
        pl.semaphore_signal(barrier, inc=1, device_id={axis: index}, device_id_type=MESH)

    greet("gx", partner)
    pl.when(has_out)(lambda: greet("gx", outward))
    pl.when(has_in)(lambda: greet("gx", inward))
    pl.when(has_low)(lambda: greet("gy", iy - 1))
    pl.when(has_high)(lambda: greet("gy", iy + 1))

    for wide in wides:
        for field in range(2):

            @pl.when(jnp.logical_not(has_in))
            def _():
                wide[field, core, near_at, :] = jnp.zeros((cells_y, cells_x, LANES), jnp.float32)

            @pl.when(jnp.logical_not(has_out))
            def _():
                wide[field, core, far_at, :] = jnp.zeros((cells_y, cells_x, LANES), jnp.float32)

            edge = jnp.zeros((RADIUS, 4 * cells_x, LANES), jnp.float32)

            @pl.when(jnp.logical_not(has_low))
            def _():
                wide[field, pl.ds(0, RADIUS)] = edge

            @pl.when(jnp.logical_not(has_high))
            def _():
                wide[field, pl.ds(cells_y + RADIUS, RADIUS)] = edge

    pl.semaphore_wait(
        barrier,
        1 + sum(flag.astype(jnp.int32) for flag in (has_out, has_in, has_low, has_high)),
    )

    def remote(pair, kind, src, dst, axis, index):
        return pltpu.make_async_remote_copy(
            src_ref=src,
            dst_ref=dst,
            send_sem=send_sem.at[pair, kind],
            recv_sem=recv_sem.at[pair, kind],
            device_id={axis: index},
            device_id_type=MESH,
        )

    def swap_copy(pair):
        dst = wides[pair].at[:, core, own_at, :]
        return remote(pair, SWAP, sent.at[pair], dst, "gx", partner)

    def swap_arrival(pair):
        dst = wides[pair].at[:, core, recv_at, :]
        return remote(pair, SWAP, sent.at[pair], dst, "gx", partner)

    def near_copy(pair):
        return remote(
            pair, NEAR, own.at[pair], wides[pair].at[:, core, near_at, :], "gx", outward
        )

    def far_copy(pair):
        wide = wides[pair]
        return remote(
            pair,
            FAR,
            wide.at[:, core, recv_at, :],
            wide.at[:, core, far_at, :],
            "gx",
            inward,
        )

    def edge_copies(pair, kind, at):
        wide = wides[pair]
        size = RADIUS
        up = remote(
            pair,
            kind,
            wide.at[:, pl.ds(cells_y, size), at, :],
            wide.at[:, pl.ds(0, size), at, :],
            "gy",
            iy + 1,
        )
        down = remote(
            pair,
            kind + 1,
            wide.at[:, pl.ds(RADIUS, size), at, :],
            wide.at[:, pl.ds(cells_y + RADIUS, size), at, :],
            "gy",
            iy - 1,
        )
        return up, down

    def start_edges(pair, kind, at):
        up, down = edge_copies(pair, kind, at)
        pl.when(has_high)(up.start)
        pl.when(has_low)(down.start)

    def wait_edges(pair, kind, at):
        up, down = edge_copies(pair, kind, at)
        pl.when(has_low)(up.wait_recv)
        pl.when(has_high)(down.wait_recv)

    def own_copy(pair):
        return pltpu.make_async_copy(
            own.at[pair], wides[pair].at[:, core, own_at, :], own_sem.at[pair]
        )

    def out_copy(pair, field):
        return remote(
            pair,
            OUT + field,
            stages[pair].at[1, field],
            outs[field].at[pair, :, lane_at],
            "gx",
            partner,
        )

    def out_arrival(pair, field):
        theirs = pl.ds(pl.multiple_of((1 - parity) * LANES, LANES), LANES)
        return remote(
            pair,
            OUT + field,
            stages[pair].at[1, field],
            outs[field].at[pair, :, theirs],
            "gx",
            partner,
        )

    def mine_copy(pair, field):
        return pltpu.make_async_copy(
            stages[pair].at[0, field],
            outs[field].at[pair, :, lane_at],
            mine_sem.at[pair, field],
        )

    def compute(pair, side, field):
        wide, stage = wides[pair], stages[pair]
        rows = cells_y + 2 * RADIUS
        row = rows_of[pair]
        upper = side + parity - 2 * side * parity

        sign = 2 - 4 * field

        @pl.loop(0, blocks)
        def _(block):
            base = cells_x + upper * cells_x + block * SUB
            at = pl.ds(pl.multiple_of(base, SUB), SUB)
            centre = [wide[field, y, at, :] for y in range(rows)]

            def term(h, totals):
                moved = pl.ds(base + sign * lags[h], SUB)
                weight = weights[row, h] * 0.0625
                other = [wide[1 - field, y, moved, :] for y in range(rows)]
                image = smooth_rows([c * o for c, o in zip(centre, other)])
                return tuple(
                    total + (weight * value) * o
                    for total, value, o in zip(totals, image, other[RADIUS:])
                )

            zeros = tuple(jnp.zeros((SUB, LANES), jnp.float32) for _ in range(cells_y))
            totals = lax.fori_loop(0, noff, term, zeros)
            first = block * SUB * cells_y
            for y in range(cells_y):
                stage[side, field, pl.ds(first + y, SUB, stride=cells_y), :] = totals[y]

    pairs = range(pair_count)
    for pair in pairs:
        swap_copy(pair).start()
        pl.when(has_out)(near_copy(pair).start)
    for pair in pairs:
        own_copy(pair).start()
    for pair in pairs:
        own_copy(pair).wait()

    def forward(pair):
        swap_arrival(pair).wait_recv()
        pl.when(has_in)(far_copy(pair).start)
        pl.when(has_in)(near_copy(pair).wait_recv)
        start_edges(pair, REST_UP, rest_at)

    def finish(pair):
        pl.when(has_out)(far_copy(pair).wait_recv)
        start_edges(pair, FAR_UP, far_at)

    def settle(pair):
        wait_edges(pair, REST_UP, rest_at)
        wait_edges(pair, FAR_UP, far_at)

    forward(0)
    for pair in pairs:
        if pair + 1 < pair_count:
            forward(pair + 1)
        finish(pair)
        settle(pair)
        for field in range(2):
            compute(pair, 1, field)
            out_copy(pair, field).start()
        for field in range(2):
            compute(pair, 0, field)
            mine_copy(pair, field).start()

    for pair in pairs:
        swap_copy(pair).wait_send()
        pl.when(has_out)(near_copy(pair).wait_send)
        pl.when(has_in)(far_copy(pair).wait_send)
        for kind, at in ((REST_UP, rest_at), (FAR_UP, far_at)):
            up, down = edge_copies(pair, kind, at)
            pl.when(has_high)(up.wait_send)
            pl.when(has_low)(down.wait_send)
        for field in range(2):
            mine_copy(pair, field).wait()
            out_copy(pair, field).wait_send()
            out_arrival(pair, field).wait_recv()


def local(source_snaps, receiver_snaps, snap_pairs, offset_lags, weight_table, weight_index):
    _, cells_x, cells_y, depth = source_snaps.shape
    pair_count = snap_pairs.shape[0]
    own, sent = gather(snap_pairs, source_snaps, receiver_snaps)
    smem = pl.BlockSpec(memory_space=pltpu.SMEM)
    anywhere = pl.BlockSpec(memory_space=pl.ANY)
    wide = pltpu.VMEM((2, cells_y + 2 * RADIUS, 4 * cells_x, LANES), jnp.float32)
    stage = pltpu.VMEM((2, 2, cells_x * cells_y, LANES), jnp.float32)
    out = pl.pallas_call(
        functools.partial(adjoint_kernel, lax.axis_size("gx"), lax.axis_size("gy")),
        out_shape=[
            jax.ShapeDtypeStruct((pair_count, cells_x * cells_y, depth), jnp.float32)
        ] * 2,
        in_specs=[smem] * 3 + [pl.BlockSpec(memory_space=pltpu.HBM)] * 2,
        out_specs=[anywhere] * 2,
        scratch_shapes=[wide] * pair_count
        + [stage] * pair_count
        + [
            pltpu.SemaphoreType.DMA((pair_count, KINDS)),
            pltpu.SemaphoreType.DMA((pair_count, KINDS)),
            pltpu.SemaphoreType.DMA((pair_count,)),
            pltpu.SemaphoreType.DMA((pair_count, 2)),
        ],
        compiler_params=pltpu.CompilerParams(
            collective_id=0, has_side_effects=True, vmem_limit_bytes=48 * 1024 * 1024
        ),
        name="adjoints",
    )(offset_lags, weight_table, weight_index, own, sent)
    return tuple(a.reshape(pair_count, cells_x, cells_y, depth) for a in out)


def solution(mesh):
    return jax.shard_map(
        local,
        mesh=mesh,
        in_specs=(P(None, "gx", "gy", None), P(None, "gx", "gy", None), P(), P(), P(), P()),
        out_specs=(P(None, "gx", "gy", None), P(None, "gx", "gy", None)),
        check_vma=False,
    )
```
